32 devices in a mesh: grp: 4 (over x, core), node: 8 (over z, y).
Axes of the slice: x: 2, y: 2, z: 4, core: 2. Of those that a mesh axis runs over, the one named last changes fastest.
Arguments:
- samples: bfloat16 [16384, 512], P(('grp', 'node')), may hold values from -6 to 6
- omega: bfloat16 [16384, 512], P(('grp', 'node')), may hold values from -6 to 6
- diag_block: bfloat16 [16384, 512], P(('grp', 'node')), may hold values from -0.25 to 0.25
- leaf_pivots: int32 [32, 128], P(('grp', 'node')), may hold values from 0 to 511, as said below
- leaf_interp: bfloat16 [16384, 128], P(('grp', 'node')), may hold values from -0.25 to 0.25
- coupling: bfloat16 [4096, 128], P(('grp', 'node')), may hold values from -0.5 to 0.5
- parent_pivots: int32 [16, 128], P('grp'), may hold values from 0 to 255, as said below
- parent_interp: bfloat16 [4096, 128], P(('grp', 'node')), may hold values from -8 to 8
- far_coupling: bfloat16 [16384, 1024], P(('grp', 'node')), may hold values from -0.1875 to 0.1875
Outputs:
- parent_rows: bfloat16 [2048, 512], P(('grp', 'node'))
- transfer: bfloat16 [16384, 128], P(('grp', 'node'))
- far_field: bfloat16 [16384, 512], P(('grp', 'node'))
The draws below stay inside these ranges and needn't reach their ends.
Inputs may be any that keep to these rules, and one draw needn't show every extreme that they name: `leaf_pivots`: the 128 entries of a row are distinct local row numbers of the leaf. `parent_pivots`: the 128 entries of a row are distinct.
All inputs are finite; a program needn't handle non-finite values.
Results may differ from the reference program's by a relative error of at most 0.01.
Values may be sent and summed in bfloat16 or wider, within the bound.
A program may use at most 64 MiB of HBM per device.

```python
import jax
import jax.numpy as jnp
from jax import lax

M = 512
K = 128
S = 512
N = 16384
GROUP_ROWS = 512
PARENT_ROWS = 2048
N_GRP = 4
N_NODE = 8


def pick_distinct(key, row_count, value_count, pick_count):
    row_keys = jax.random.split(key, row_count)

    def pick_row(row_key):
        key_order, key_shuffle = jax.random.split(row_key)
        order = jax.random.permutation(key_order, value_count)
        where_top = jnp.argmax(order == value_count - 1)
        order = order.at[where_top].set(order[0]).at[0].set(value_count - 1)
        chosen = jax.random.permutation(key_shuffle, order[:pick_count])
        return chosen.astype(jnp.int32)
    return jax.vmap(pick_row)(row_keys)


def draw_leaf_pivots(key, part):
    return pick_distinct(jax.random.fold_in(key, 11), N_GRP * N_NODE, M, K)


def draw_parent_pivots(key, part):
    return pick_distinct(jax.random.fold_in(key, 23), N_GRP * N_NODE // 2, 2 * K, K)


def block_scale(stream_key, extent, cuts, low, largest):
    loudness, own = 1.0, jax.random.fold_in(stream_key, 6)
    for axis_at, parts in cuts:
        steps = jnp.exp(jax.random.uniform(jax.random.fold_in(own, axis_at), (parts,), jnp.float32, low / len(cuts), largest / len(cuts)))
        loudness = loudness * jnp.repeat(steps, extent[axis_at] // parts).reshape([-1 if axis == axis_at else 1 for axis in range(len(extent))])
    return loudness


def gaussian(stream_key, shape, width, most, cuts=(), dtype=jnp.bfloat16):
    level = block_scale(stream_key, shape, cuts, -0.22, 0.18) if cuts else 1.0
    values = jax.random.normal(stream_key, shape, jnp.float32) * width * level
    return jnp.minimum(jnp.maximum(values, -most), most).astype(dtype)


def setup_inputs(seed: int = 0) -> dict:
    splits = jax.random.split(jax.random.key(seed), 10)
    return {
        "samples": gaussian(splits[0], (N, S), 1.0, 6.0, ((0, 32),)),
        "omega": gaussian(splits[1], (N, S), 1.0, 6.0, ((0, 32),)),
        "diag_block": gaussian(splits[2], (N, M), M ** -0.5, 0.25, ((0, 32),)),
        "leaf_pivots": draw_leaf_pivots(jax.random.fold_in(splits[9], 71), 0),
        "leaf_interp": gaussian(splits[4], (N, K), M ** -0.5, 0.25, ((0, 32),)),
        "coupling": gaussian(splits[5], (N_GRP * N_NODE * K, K), K ** -0.5, 0.5, ((0, 32),)),
        "parent_pivots": draw_parent_pivots(jax.random.fold_in(splits[9], 71), 0),
        "parent_interp": gaussian(splits[7], (N_GRP * N_NODE * K, K), 2.0, 8.0, ((0, 32),)),
        "far_coupling": gaussian(splits[8], (N, 2 * GROUP_ROWS), (2 * GROUP_ROWS) ** -0.5, 0.1875, ((0, 32),)),
    }


def reference(samples, omega, diag_block, leaf_pivots, leaf_interp, coupling, parent_pivots, parent_interp, far_coupling):
    leaves = N_GRP * N_NODE
    sample_blocks = samples.reshape(leaves, M, S)
    omega_blocks = omega.reshape(leaves, M, S)
    diag_blocks = diag_block.reshape(leaves, M, M)
    picked_diag = jnp.take_along_axis(diag_blocks, leaf_pivots[:, :, None], axis=1)
    picked_rows = jnp.take_along_axis(sample_blocks, leaf_pivots[:, :, None], axis=1)
    skeleton = (picked_rows.astype(jnp.float32) - jnp.einsum("lkm,lms->lks", picked_diag.astype(jnp.float32), omega_blocks.astype(jnp.float32))).astype(jnp.bfloat16)
    interp_blocks = leaf_interp.reshape(leaves, M, K)
    compressed = jnp.einsum("lmk,lms->lks", interp_blocks.astype(jnp.float32), omega_blocks.astype(jnp.float32)).astype(jnp.bfloat16)
    sibling_basis = compressed.reshape(leaves // 2, 2, K, S)[:, ::-1].reshape(leaves, K, S)
    coupling_blocks = coupling.reshape(leaves, K, K)
    reduced = (skeleton.astype(jnp.float32) - jnp.einsum("lkj,ljs->lks", coupling_blocks.astype(jnp.float32), sibling_basis.astype(jnp.float32))).astype(jnp.bfloat16)
    merged = reduced.reshape(leaves // 2, 2 * K, S)
    parent = jnp.take_along_axis(merged, parent_pivots[:, :, None], axis=1)
    parent_rows = parent.reshape(PARENT_ROWS, S)
    parent_blocks = parent_interp.reshape(leaves, K, K)
    transfer = jnp.einsum("lmk,lkj->lmj", interp_blocks.astype(jnp.float32), parent_blocks.astype(jnp.float32)).astype(jnp.bfloat16).reshape(N, K)
    groups = parent.reshape(N_GRP, GROUP_ROWS, S)
    sibling_rows = groups.reshape(N_GRP // 2, 2, GROUP_ROWS, S)[:, ::-1].reshape(N_GRP, GROUP_ROWS, S)
    stacked = jnp.concatenate([groups, sibling_rows], axis=1)
    far_blocks = far_coupling.reshape(N_GRP, N_NODE * M, 2 * GROUP_ROWS)

    def product(operands):
        return jnp.dot(operands[0], operands[1], preferred_element_type=jnp.float32).astype(jnp.bfloat16)

    far_field = lax.map(product, (far_blocks, stacked)).reshape(N, S)
    return parent_rows, transfer, far_field
```

```python
import functools

import jax
import jax.numpy as jnp
from jax import lax
from jax.experimental import pallas as pl
from jax.experimental.pallas import tpu as pltpu
from jax.sharding import PartitionSpec as P

MESH = pl.DeviceIdType.MESH
F32 = jnp.float32
BF16 = jnp.bfloat16


def tdot(a, b):
    return lax.dot_general(a, b, (((0,), (0,)), ((), ())), preferred_element_type=F32)


def dot(a, b):
    return jnp.dot(a, b, preferred_element_type=F32)


def partner(pair, d, pairs):
    if pairs & (pairs - 1):
        return lax.rem(pair + d, pairs)
    out, bit = pair, 1
    while bit < pairs:
        if d & bit:
            out = out + bit - 2 * bit * lax.rem(pair // bit, 2)
        bit *= 2
    return out


def kernel(
    pairs,
    chunks,
    samples,
    omega,
    diag,
    leaf_piv,
    interp,
    coupling,
    par_piv,
    par_interp,
    far,
    rows_out,
    transfer_out,
    far_out,
    samples_v,
    omega_v,
    diag_v,
    interp_v,
    coup_v,
    par_interp_v,
    far_v,
    u_mine,
    u_sib,
    own_q,
    sib_q,
    rows_v,
    transfer_v,
    far_o,
    load_sem,
    coup_sem,
    u_sem,
    z_send,
    z_recv,
    y_send,
    y_recv,
    c_send,
    c_recv,
    p_sem,
    out_sem,
):
    grp, node = lax.axis_index("grp"), lax.axis_index("node")
    pair, parity = node // 2, lax.rem(node, 2)
    node_sib = node + 1 - 2 * parity
    grp_sib = grp + 1 - 2 * lax.rem(grp, 2)
    rank = leaf_piv.shape[1]
    half = rank // 2
    m = omega.shape[0]
    width = omega.shape[1] // chunks
    others = [partner(pair, d, pairs) for d in range(1, pairs)]

    barrier = pltpu.get_barrier_semaphore()
    pl.semaphore_signal(barrier, inc=1, device_id=(grp, node_sib), device_id_type=MESH)
    pl.semaphore_signal(barrier, inc=1, device_id=(grp_sib, node), device_id_type=MESH)
    for other in others:
        pl.semaphore_signal(
            barrier, inc=1, device_id=(grp, 2 * other + parity), device_id_type=MESH
        )

    loads = []
    for at, (src, dst) in enumerate(
        (
            (interp, interp_v),
            (omega, omega_v),
            (diag, diag_v),
            (samples, samples_v),
            (par_interp, par_interp_v),
            (far, far_v),
        )
    ):
        loads.append(pltpu.make_async_copy(src, dst, load_sem.at[at]))
        loads[-1].start()

    pl.semaphore_wait(barrier, pairs + 1)

    def remote(src, dst, send, recv, where):
        return pltpu.make_async_remote_copy(
            src_ref=src,
            dst_ref=dst,
            send_sem=send,
            recv_sem=recv,
            device_id=where,
            device_id_type=MESH,
        )

    sent = []

    def send(src, dst, s, r, where):
        copy = remote(src, dst, s, r, where)
        copy.start()
        sent.append(copy)
        return copy

    coup_copy = send(coupling, coup_v, coup_sem.at[0], coup_sem.at[1], (grp, node_sib))

    leaf_sel = (lax.broadcasted_iota(jnp.int32, (m, rank), 0) == leaf_piv[...]).astype(F32).astype(BF16)
    slots = par_piv[pl.ds(pair, 1), :]
    rows = lax.broadcasted_iota(jnp.int32, (rank, rank), 0)
    own_sel = (rows + parity * rank == slots).astype(F32).astype(BF16)
    sib_sel = (rows + (1 - parity) * rank == slots).astype(F32).astype(BF16)
    pick = dot(leaf_sel, own_sel).astype(BF16)

    loads[0].wait()
    loads[1].wait()
    compressed = tdot(interp_v[...], omega_v[...]).astype(BF16)
    loads[2].wait()
    diag_rows = tdot(pick, diag_v[...]).astype(BF16)
    loads[3].wait()
    skeleton = tdot(pick, samples_v[...]) - dot(diag_rows, omega_v[...])
    coup_copy.wait_recv()
    coup_rows = tdot(sib_sel, coup_v[...]).astype(BF16)
    u_copies = []
    for k in range(chunks):
        cols = slice(k * width, (k + 1) * width)
        u_mine[k] = (skeleton[:, cols] - dot(coup_rows, compressed[:, cols])).astype(BF16)
        u_copies.append(
            send(u_mine.at[k], u_sib.at[k], u_sem.at[0, k], u_sem.at[1, k], (grp, node_sib))
        )

    loads[4].wait()
    transfer_v[...] = dot(interp_v[...], par_interp_v[...]).astype(BF16)
    outs = [pltpu.make_async_copy(transfer_v, transfer_out, out_sem.at[0])]
    outs[0].start()

    def place(q, k, p, h=None):
        if h is None:
            return q.at[k, pl.ds(pl.multiple_of(p * rank, rank), rank), :]
        return q.at[k, pl.ds(pl.multiple_of(p * rank + h * half, half), half), :]

    p_copies = []
    for k in range(chunks):
        cols = slice(k * width, (k + 1) * width)
        u_copies[k].wait_recv()
        merged = (u_mine[k].astype(F32) + u_sib[k].astype(F32)).astype(BF16)
        own_q[k, pl.ds(pl.multiple_of(pair * rank, rank), rank), :] = merged
        spot = place(own_q, k, pair, parity)
        for other in others:
            send(
                spot,
                spot,
                z_send.at[k, other],
                z_recv.at[k, pair],
                (grp, 2 * other + parity),
            )
        p_copies.append(
            send(
                place(own_q, k, pair),
                place(sib_q, k, pair),
                p_sem.at[0, k],
                p_sem.at[1, k],
                (grp_sib, node),
            )
        )
        rows_v[:, cols] = own_q[
            k, pl.ds(pl.multiple_of(pair * rank + parity * half, half), half), :
        ]
    outs.append(pltpu.make_async_copy(rows_v, rows_out, out_sem.at[1]))
    outs[1].start()

    for k in range(chunks):
        for other in others:
            spot = place(own_q, k, other, parity)
            remote(
                spot, spot, z_send.at[k, other], z_recv.at[k, other], (grp, node_sib)
            ).wait_recv()
            send(spot, spot, y_send.at[k, other], y_recv.at[k, other], (grp, node_sib))
            send(
                spot,
                place(sib_q, k, other, parity),
                c_send.at[k, other, 0],
                c_recv.at[k, other, 0],
                (grp_sib, node),
            )

    loads[5].wait()
    own_width = far.shape[1] // 2
    parts = []
    for k in range(chunks):
        for other in others:
            spot = place(own_q, k, other, 1 - parity)
            remote(
                spot, spot, y_send.at[k, other], y_recv.at[k, other], (grp, node_sib)
            ).wait_recv()
            send(
                spot,
                place(sib_q, k, other, 1 - parity),
                c_send.at[k, other, 1],
                c_recv.at[k, other, 1],
                (grp_sib, node),
            )
        far_o[k] = dot(far_v[:, :own_width], own_q[k])
    for k in range(chunks):
        cols = slice(k * width, (k + 1) * width)
        p_copies[k].wait_recv()
        for other in others:
            for h in range(2):
                spot = place(sib_q, k, other, parity + h - 2 * parity * h)
                remote(
                    spot,
                    spot,
                    c_send.at[k, other, h],
                    c_recv.at[k, other, h],
                    (grp_sib, node),
                ).wait_recv()
        samples_v[:, cols] = (far_o[k] + dot(far_v[:, own_width:], sib_q[k])).astype(BF16)
        copy = pltpu.make_async_copy(
            samples_v.at[:, pl.ds(k * width, width)],
            far_out.at[:, pl.ds(k * width, width)],
            out_sem.at[2 + k],
        )
        copy.start()
        outs.append(copy)
    for copy in sent:
        copy.wait_send()
    for copy in outs:
        copy.wait()


def shards(chunks, *args):
    samples, omega, diag, leaf_piv, interp, coupling, par_piv, par_interp, far = args
    pairs = lax.axis_size("node") // 2
    rank = leaf_piv.shape[1]
    m, s = omega.shape
    width = s // chunks
    group = pairs * rank
    anywhere = pl.BlockSpec(memory_space=pl.ANY)
    vmem = pl.BlockSpec(memory_space=pltpu.VMEM)
    dma = pltpu.SemaphoreType.DMA
    return pl.pallas_call(
        functools.partial(kernel, pairs, chunks),
        out_shape=(
            jax.ShapeDtypeStruct((rank // 2, s), BF16),
            jax.ShapeDtypeStruct((m, rank), BF16),
            jax.ShapeDtypeStruct((m, s), BF16),
        ),
        in_specs=[anywhere, anywhere, anywhere, vmem, anywhere, anywhere, vmem, anywhere, anywhere],
        out_specs=(anywhere, anywhere, anywhere),
        scratch_shapes=[
            pltpu.VMEM((m, s), BF16),
            pltpu.VMEM((m, s), BF16),
            pltpu.VMEM((m, m), BF16),
            pltpu.VMEM((m, rank), BF16),
            pltpu.VMEM((rank, rank), BF16),
            pltpu.VMEM((rank, rank), BF16),
            pltpu.VMEM(far.shape, BF16),
            pltpu.VMEM((chunks, rank, width), BF16),
            pltpu.VMEM((chunks, rank, width), BF16),
            pltpu.VMEM((chunks, group, width), BF16),
            pltpu.VMEM((chunks, group, width), BF16),
            pltpu.VMEM((rank // 2, s), BF16),
            pltpu.VMEM((m, rank), BF16),
            pltpu.VMEM((chunks, m, width), F32),
            dma((6,)),
            dma((2,)),
            dma((2, chunks)),
            dma((chunks, pairs)),
            dma((chunks, pairs)),
            dma((chunks, pairs)),
            dma((chunks, pairs)),
            dma((chunks, pairs, 2)),
            dma((chunks, pairs, 2)),
            dma((2, chunks)),
            dma((2 + chunks,)),
        ],
        compiler_params=pltpu.CompilerParams(
            collective_id=0, has_side_effects=True, vmem_limit_bytes=60 * 1024 * 1024
        ),
        name="merge_level",
    )(*args)


def solution(mesh):
    split = P(("grp", "node"), None)
    return jax.shard_map(
        functools.partial(shards, 2),
        mesh=mesh,
        in_specs=(split, split, split, split, split, split, P("grp", None), split, split),
        out_specs=(split, split, split),
        check_vma=False,
    )
```

```python
import functools

import jax
import jax.numpy as jnp
from jax import lax
from jax.experimental import pallas as pl
from jax.experimental.pallas import tpu as pltpu
from jax.sharding import PartitionSpec as P

MESH = pl.DeviceIdType.MESH
F32 = jnp.float32
BF16 = jnp.bfloat16


def tdot(a, b):
    return lax.dot_general(a, b, (((0,), (0,)), ((), ())), preferred_element_type=F32)


def dot(a, b):
    return jnp.dot(a, b, preferred_element_type=F32)


def partner(pair, d, pairs):
    if pairs & (pairs - 1):
        return lax.rem(pair + d, pairs)
    out, bit = pair, 1
    while bit < pairs:
        if d & bit:
            out = out + bit - 2 * bit * lax.rem(pair // bit, 2)
        bit *= 2
    return out


def kernel(
    pairs,
    chunks,
    samples,
    omega,
    diag,
    leaf_piv,
    interp,
    coupling,
    par_piv,
    par_interp,
    far,
    rows_v,
    transfer_v,
    far_done,
    samples_v,
    omega_v,
    diag_v,
    interp_v,
    coup_v,
    par_interp_v,
    far_v,
    u_mine,
    u_sib,
    own_q,
    sib_q,
    far_o,
    load_sem,
    coup_sem,
    u_sem,
    z_send,
    z_recv,
    y_send,
    y_recv,
    c_send,
    c_recv,
    p_sem,
):
    grp, node = lax.axis_index("grp"), lax.axis_index("node")
    pair, parity = node // 2, lax.rem(node, 2)
    node_sib = node + 1 - 2 * parity
    grp_sib = grp + 1 - 2 * lax.rem(grp, 2)
    rank = leaf_piv.shape[1]
    half = rank // 2
    m = omega.shape[0]
    width = omega.shape[1] // chunks
    others = [partner(pair, d, pairs) for d in range(1, pairs)]

    barrier = pltpu.get_barrier_semaphore()
    pl.semaphore_signal(barrier, inc=1, device_id=(grp, node_sib), device_id_type=MESH)
    pl.semaphore_signal(barrier, inc=1, device_id=(grp_sib, node), device_id_type=MESH)
    for other in others:
        pl.semaphore_signal(
            barrier, inc=1, device_id=(grp, 2 * other + parity), device_id_type=MESH
        )

    loads = []
    for at, (src, dst) in enumerate(
        (
            (interp, interp_v),
            (omega, omega_v),
            (diag, diag_v),
            (samples, samples_v),
            (par_interp, par_interp_v),
            (far, far_v),
        )
    ):
        loads.append(pltpu.make_async_copy(src, dst, load_sem.at[at]))
        loads[-1].start()

    pl.semaphore_wait(barrier, pairs + 1)

    def remote(src, dst, send, recv, where):
        return pltpu.make_async_remote_copy(
            src_ref=src,
            dst_ref=dst,
            send_sem=send,
            recv_sem=recv,
            device_id=where,
            device_id_type=MESH,
        )

    sent = []

    def send(src, dst, s, r, where):
        copy = remote(src, dst, s, r, where)
        copy.start()
        sent.append(copy)
        return copy

    coup_copy = send(coupling, coup_v, coup_sem.at[0], coup_sem.at[1], (grp, node_sib))

    leaf_sel = (lax.broadcasted_iota(jnp.int32, (m, rank), 0) == leaf_piv[...]).astype(F32).astype(BF16)
    slots = par_piv[pl.ds(pair, 1), :]
    rows = lax.broadcasted_iota(jnp.int32, (rank, rank), 0)
    own_sel = (rows + parity * rank == slots).astype(F32).astype(BF16)
    sib_sel = (rows + (1 - parity) * rank == slots).astype(F32).astype(BF16)
    pick = dot(leaf_sel, own_sel).astype(BF16)

    loads[0].wait()
    loads[1].wait()
    compressed = tdot(interp_v[...], omega_v[...]).astype(BF16)
    loads[2].wait()
    diag_rows = tdot(pick, diag_v[...]).astype(BF16)
    loads[3].wait()
    skeleton = tdot(pick, samples_v[...]) - dot(diag_rows, omega_v[...])
    coup_copy.wait_recv()
    coup_rows = tdot(sib_sel, coup_v[...]).astype(BF16)
    u_copies = []
    for k in range(chunks):
        cols = slice(k * width, (k + 1) * width)
        u_mine[k] = (skeleton[:, cols] - dot(coup_rows, compressed[:, cols])).astype(BF16)
        u_copies.append(
            send(u_mine.at[k], u_sib.at[k], u_sem.at[0, k], u_sem.at[1, k], (grp, node_sib))
        )

    loads[4].wait()
    transfer_v[...] = dot(interp_v[...], par_interp_v[...]).astype(BF16)

    def place(q, k, p, h=None):
        if h is None:
            return q.at[k, pl.ds(pl.multiple_of(p * rank, rank), rank), :]
        return q.at[k, pl.ds(pl.multiple_of(p * rank + h * half, half), half), :]

    p_copies = []
    for k in range(chunks):
        cols = slice(k * width, (k + 1) * width)
        u_copies[k].wait_recv()
        merged = (u_mine[k].astype(F32) + u_sib[k].astype(F32)).astype(BF16)
        own_q[k, pl.ds(pl.multiple_of(pair * rank, rank), rank), :] = merged
        spot = place(own_q, k, pair, parity)
        for other in others:
            send(
                spot,
                spot,
                z_send.at[k, other],
                z_recv.at[k, pair],
                (grp, 2 * other + parity),
            )
        p_copies.append(
            send(
                place(own_q, k, pair),
                place(sib_q, k, pair),
                p_sem.at[0, k],
                p_sem.at[1, k],
                (grp_sib, node),
            )
        )
        rows_v[:, cols] = own_q[
            k, pl.ds(pl.multiple_of(pair * rank + parity * half, half), half), :
        ]

    for k in range(chunks):
        for other in others:
            spot = place(own_q, k, other, parity)
            remote(
                spot, spot, z_send.at[k, other], z_recv.at[k, other], (grp, node_sib)
            ).wait_recv()
            send(spot, spot, y_send.at[k, other], y_recv.at[k, other], (grp, node_sib))
            send(
                spot,
                place(sib_q, k, other, parity),
                c_send.at[k, other, 0],
                c_recv.at[k, other, 0],
                (grp_sib, node),
            )

    loads[5].wait()
    own_width = far.shape[1] // 2
    parts = []
    for k in range(chunks):
        for other in others:
            spot = place(own_q, k, other, 1 - parity)
            remote(
                spot, spot, y_send.at[k, other], y_recv.at[k, other], (grp, node_sib)
            ).wait_recv()
            send(
                spot,
                place(sib_q, k, other, 1 - parity),
                c_send.at[k, other, 1],
                c_recv.at[k, other, 1],
                (grp_sib, node),
            )
        far_o[k] = dot(far_v[:, :own_width], own_q[k])
    for k in range(chunks):
        cols = slice(k * width, (k + 1) * width)
        p_copies[k].wait_recv()
        for other in others:
            for h in range(2):
                spot = place(sib_q, k, other, parity + h - 2 * parity * h)
                remote(
                    spot,
                    spot,
                    c_send.at[k, other, h],
                    c_recv.at[k, other, h],
                    (grp_sib, node),
                ).wait_recv()
        far_done[:, cols] = (far_o[k] + dot(far_v[:, own_width:], sib_q[k])).astype(BF16)
    for copy in sent:
        copy.wait_send()


def emit(*refs):
    count = len(refs) // 2
    sem = refs[-1]
    copies = [
        pltpu.make_async_copy(refs[at], refs[count + at], sem.at[at]) for at in range(count)
    ]
    for copy in copies:
        copy.start()
    for copy in copies:
        copy.wait()


def shards(chunks, *args):
    samples, omega, diag, leaf_piv, interp, coupling, par_piv, par_interp, far = args
    pairs = lax.axis_size("node") // 2
    rank = leaf_piv.shape[1]
    m, s = omega.shape
    width = s // chunks
    group = pairs * rank
    hbm = pl.BlockSpec(memory_space=pltpu.HBM)
    vmem = pl.BlockSpec(memory_space=pltpu.VMEM)
    dma = pltpu.SemaphoreType.DMA
    shapes = ((rank // 2, s), (m, rank), (m, s))
    held = pl.pallas_call(
        functools.partial(kernel, pairs, chunks),
        out_shape=tuple(pltpu.VMEM(shape, BF16) for shape in shapes),
        in_specs=[hbm, hbm, hbm, vmem, hbm, hbm, vmem, hbm, hbm],
        out_specs=(vmem, vmem, vmem),
        scratch_shapes=[
            pltpu.VMEM((m, s), BF16),
            pltpu.VMEM((m, s), BF16),
            pltpu.VMEM((m, m), BF16),
            pltpu.VMEM((m, rank), BF16),
            pltpu.VMEM((rank, rank), BF16),
            pltpu.VMEM((rank, rank), BF16),
            pltpu.VMEM(far.shape, BF16),
            pltpu.VMEM((chunks, rank, width), BF16),
            pltpu.VMEM((chunks, rank, width), BF16),
            pltpu.VMEM((chunks, group, width), BF16),
            pltpu.VMEM((chunks, group, width), BF16),
            pltpu.VMEM((chunks, m, width), F32),
            dma((6,)),
            dma((2,)),
            dma((2, chunks)),
            dma((chunks, pairs)),
            dma((chunks, pairs)),
            dma((chunks, pairs)),
            dma((chunks, pairs)),
            dma((chunks, pairs, 2)),
            dma((chunks, pairs, 2)),
            dma((2, chunks)),
        ],
        compiler_params=pltpu.CompilerParams(
            collective_id=0, has_side_effects=True, vmem_limit_bytes=60 * 1024 * 1024
        ),
        name="merge_level",
    )(*args)
    return pl.pallas_call(
        emit,
        out_shape=tuple(jax.ShapeDtypeStruct(shape, BF16) for shape in shapes),
        in_specs=[pl.BlockSpec(memory_space=pl.ANY)] * len(shapes),
        out_specs=(hbm,) * len(shapes),
        scratch_shapes=[dma((len(shapes),))],
        name="emit",
    )(*(pltpu.with_memory_space_constraint(block, pltpu.VMEM) for block in held))


def solution(mesh):
    split = P(("grp", "node"), None)
    return jax.shard_map(
        functools.partial(shards, 2),
        mesh=mesh,
        in_specs=(split, split, split, split, split, split, P("grp", None), split, split),
        out_specs=(split, split, split),
        check_vma=False,
    )
```

```python
import functools

import jax
import jax.numpy as jnp
from jax import lax
from jax.experimental import pallas as pl
from jax.experimental.pallas import tpu as pltpu
from jax.sharding import PartitionSpec as P

MESH = pl.DeviceIdType.MESH
F32 = jnp.float32
BF16 = jnp.bfloat16


def tdot(a, b):
    return lax.dot_general(a, b, (((0,), (0,)), ((), ())), preferred_element_type=F32)


def dot(a, b):
    return jnp.dot(a, b, preferred_element_type=F32)


def kernel(
    pairs,
    chunks,
    samples,
    omega,
    diag,
    leaf_piv,
    interp,
    coupling,
    par_piv,
    par_interp,
    far,
    rows_v,
    transfer_v,
    far_done,
    samples_v,
    omega_v,
    diag_v,
    interp_v,
    coup_v,
    par_interp_v,
    far_v,
    u_mine,
    u_sib,
    own_q,
    sib_q,
    far_o,
    load_sem,
    coup_sem,
    u_sem,
    z_send,
    z_recv,
    y_send,
    y_recv,
    c_send,
    c_recv,
    ready,
):
    grp, node = lax.axis_index("grp"), lax.axis_index("node")
    pair, parity = node // 2, lax.rem(node, 2)
    node_sib = node + 1 - 2 * parity
    grp_sib = grp + 1 - 2 * lax.rem(grp, 2)
    rank = leaf_piv.shape[1]
    half = rank // 2
    m = omega.shape[0]
    width = omega.shape[1] // chunks
    below, above = pair > 0, pair < pairs - 1
    lower, upper = (grp, node - 2), (grp, node + 2)

    barrier = pltpu.get_barrier_semaphore()

    def greet(where):
        pl.semaphore_signal(barrier, inc=1, device_id=where, device_id_type=MESH)

    greet((grp, node_sib))
    greet((grp_sib, node))
    pl.when(below)(lambda: greet(lower))
    pl.when(above)(lambda: greet(upper))

    loads = []
    for at, (src, dst) in enumerate(
        (
            (interp, interp_v),
            (omega, omega_v),
            (diag, diag_v),
            (samples, samples_v),
            (par_interp, par_interp_v),
            (far, far_v),
        )
    ):
        loads.append(pltpu.make_async_copy(src, dst, load_sem.at[at]))
    for load in loads[:4]:
        load.start()

    greeted = 2 + (pair + pairs - 1) // pairs + (2 * pairs - 2 - pair) // pairs
    pl.semaphore_wait(barrier, greeted)

    def remote(src, dst, send, recv, where):
        return pltpu.make_async_remote_copy(
            src_ref=src,
            dst_ref=dst,
            send_sem=send,
            recv_sem=recv,
            device_id=where,
            device_id_type=MESH,
        )

    sent = []

    def send(*where):
        copy = remote(*where)
        copy.start()
        sent.append(copy.wait_send)
        return copy

    coup_copy = send(coupling, coup_v, coup_sem.at[0], coup_sem.at[1], (grp, node_sib))

    def at_distance(d, act):
        pl.when(pair >= d)(lambda: act(pair - d, above, upper))
        pl.when(pair + d < pairs)(lambda: act(pair + d, below, lower))

    def tell(other, onward, where):
        @pl.when(onward)
        def _():
            pl.semaphore_signal(
                ready.at[other], inc=1, device_id=where, device_id_type=MESH
            )

    def heard(other, onward, where):
        pl.semaphore_wait(ready.at[other], 1)
        tell(other, onward, where)

    at_distance(1, tell)

    leaf_sel = (lax.broadcasted_iota(jnp.int32, (m, rank), 0) == leaf_piv[...]).astype(F32).astype(BF16)
    slots = par_piv[pl.ds(pair, 1), :]
    rows = lax.broadcasted_iota(jnp.int32, (rank, rank), 0)
    own_sel = (rows + parity * rank == slots).astype(F32).astype(BF16)
    sib_sel = (rows + (1 - parity) * rank == slots).astype(F32).astype(BF16)
    pick = dot(leaf_sel, own_sel).astype(BF16)

    loads[0].wait()
    loads[1].wait()
    compressed = tdot(interp_v[...], omega_v[...]).astype(BF16)
    loads[2].wait()
    diag_rows = tdot(pick, diag_v[...]).astype(BF16)
    loads[3].wait()
    skeleton = tdot(pick, samples_v[...]) - dot(diag_rows, omega_v[...])
    coup_copy.wait_recv()
    coup_rows = tdot(sib_sel, coup_v[...]).astype(BF16)
    u_copies = []

    def theirs(k):
        return u_mine.at[k, pl.ds(pl.multiple_of((1 - parity) * half, half), half), :]

    for k in range(chunks):
        cols = slice(k * width, (k + 1) * width)
        u_mine[k] = (skeleton[:, cols] - dot(coup_rows, compressed[:, cols])).astype(BF16)
        u_copies.append(
            send(theirs(k), u_sib.at[k], u_sem.at[0, k], u_sem.at[1, k], (grp, node_sib))
        )

    loads[4].start()
    loads[5].start()
    for d in range(2, pairs):
        at_distance(d, heard)
    loads[4].wait()
    transfer_v[...] = dot(interp_v[...], par_interp_v[...]).astype(BF16)

    def place(q, k, p, h=None):
        if h is None:
            return q.at[k, pl.ds(pl.multiple_of(p * rank, rank), rank), :]
        return q.at[k, pl.ds(pl.multiple_of(p * rank + h * half, half), half), :]

    def to_z(k, other):
        spot = place(own_q, k, pair, parity)
        z_here, z_there = z_send.at[k, other], z_recv.at[k, pair]
        return remote(spot, spot, z_here, z_there, (grp, 2 * other + parity))

    def arrive(k, other, sems, h):
        spot = place(own_q, k, other, h)
        at = sems.at[k, other]
        remote(spot, spot, at, at, (grp, node_sib)).wait_recv()
        return spot

    def share(k, other, spot, h, side):
        c_here, c_there = c_send.at[k, other, side], c_recv.at[k, other, side]
        remote(spot, place(sib_q, k, other, h), c_here, c_there, (grp_sib, node)).start()

    def onward(k, other):
        spot = place(own_q, k, other, parity)
        y_here, y_there = y_send.at[k, other], y_recv.at[k, other]
        remote(spot, spot, y_here, y_there, (grp, node_sib)).start()
        share(k, other, spot, parity, 0)

    def from_z(k, other, *_):
        arrive(k, other, z_recv, parity)
        onward(k, other)

    def from_y(k, other):
        spot = arrive(k, other, y_recv, 1 - parity)
        share(k, other, spot, 1 - parity, 1)

    def drain(k, other, *_):
        spot = place(own_q, k, other, parity)
        y_here, y_there = y_send.at[k, other], y_recv.at[k, other]
        remote(spot, spot, y_here, y_there, (grp, node_sib)).wait_send()
        for side in range(2):
            c_here, c_there = c_send.at[k, other, side], c_recv.at[k, other, side]
            remote(spot, spot, c_here, c_there, (grp_sib, node)).wait_send()

    def landed(k, other, *_):
        for side in range(2):
            spot = place(sib_q, k, other, parity)
            at = c_recv.at[k, other, side]
            remote(spot, spot, at, at, (grp_sib, node)).wait_recv()

    for k in range(chunks):
        cols = slice(k * width, (k + 1) * width)
        u_copies[k].wait_recv()
        mine = u_mine[k, pl.ds(pl.multiple_of(parity * half, half), half), :]
        merged = (mine.astype(F32) + u_sib[k].astype(F32)).astype(BF16)
        own_q[k, pl.ds(pl.multiple_of(pair * rank + parity * half, half), half), :] = merged
        rows_v[:, cols] = merged
        for d in range(pairs - 1, 0, -1):
            at_distance(d, lambda other, *_: to_z(k, other).start())
        onward(k, pair)
    for k in range(chunks):
        for d in range(1, pairs):
            at_distance(d, functools.partial(from_z, k))
    loads[5].wait()
    own_width = far.shape[1] // 2
    for k in range(chunks):
        from_y(k, pair)
        for d in range(1, pairs):
            at_distance(d, lambda other, *_: from_y(k, other))
        far_o[k] = dot(far_v[:, :own_width], own_q[k])

    for k in range(chunks):
        cols = slice(k * width, (k + 1) * width)
        landed(k, pair)
        for d in range(1, pairs):
            at_distance(d, functools.partial(landed, k))
        far_done[:, cols] = (far_o[k] + dot(far_v[:, own_width:], sib_q[k])).astype(BF16)
    for wait in sent:
        wait()
    for k in range(chunks):
        drain(k, pair)
        for d in range(1, pairs):
            at_distance(d, lambda other, *_: to_z(k, other).wait_send())
            at_distance(d, functools.partial(drain, k))


def emit(*refs):
    count = len(refs) // 2
    sem = refs[-1]
    copies = [
        pltpu.make_async_copy(refs[at], refs[count + at], sem.at[at]) for at in range(count)
    ]
    for copy in copies:
        copy.start()
    for copy in copies:
        copy.wait()


def shards(chunks, *args):
    samples, omega, diag, leaf_piv, interp, coupling, par_piv, par_interp, far = args
    pairs = lax.axis_size("node") // 2
    rank = leaf_piv.shape[1]
    m, s = omega.shape
    width = s // chunks
    group = pairs * rank
    hbm = pl.BlockSpec(memory_space=pltpu.HBM)
    vmem = pl.BlockSpec(memory_space=pltpu.VMEM)
    dma = pltpu.SemaphoreType.DMA
    shapes = ((rank // 2, s), (m, rank), (m, s))
    held = pl.pallas_call(
        functools.partial(kernel, pairs, chunks),
        out_shape=tuple(pltpu.VMEM(shape, BF16) for shape in shapes),
        in_specs=[hbm, hbm, hbm, vmem, hbm, hbm, vmem, hbm, hbm],
        out_specs=(vmem, vmem, vmem),
        scratch_shapes=[
            pltpu.VMEM((m, s), BF16),
            pltpu.VMEM((m, s), BF16),
            pltpu.VMEM((m, m), BF16),
            pltpu.VMEM((m, rank), BF16),
            pltpu.VMEM((rank, rank), BF16),
            pltpu.VMEM((rank, rank), BF16),
            pltpu.VMEM(far.shape, BF16),
            pltpu.VMEM((chunks, rank, width), BF16),
            pltpu.VMEM((chunks, rank // 2, width), BF16),
            pltpu.VMEM((chunks, group, width), BF16),
            pltpu.VMEM((chunks, group, width), BF16),
            pltpu.VMEM((chunks, m, width), F32),
            dma((6,)),
            dma((2,)),
            dma((2, chunks)),
            dma((chunks, pairs)),
            dma((chunks, pairs)),
            dma((chunks, pairs)),
            dma((chunks, pairs)),
            dma((chunks, pairs, 2)),
            dma((chunks, pairs, 2)),
            pltpu.SemaphoreType.REGULAR((pairs,)),
        ],
        compiler_params=pltpu.CompilerParams(
            collective_id=0, has_side_effects=True, vmem_limit_bytes=60 * 1024 * 1024
        ),
        name="merge_level",
    )(*args)
    return pl.pallas_call(
        emit,
        out_shape=tuple(jax.ShapeDtypeStruct(shape, BF16) for shape in shapes),
        in_specs=[pl.BlockSpec(memory_space=pl.ANY)] * len(shapes),
        out_specs=(hbm,) * len(shapes),
        scratch_shapes=[dma((len(shapes),))],
        name="emit",
    )(*(pltpu.with_memory_space_constraint(block, pltpu.VMEM) for block in held))


def solution(mesh):
    split = P(("grp", "node"), None)
    return jax.shard_map(
        functools.partial(shards, 2),
        mesh=mesh,
        in_specs=(split, split, split, split, split, split, P("grp", None), split, split),
        out_specs=(split, split, split),
        check_vma=False,
    )
```

```python
import functools

import jax
import jax.numpy as jnp
from jax import lax
from jax.experimental import pallas as pl
from jax.experimental.pallas import tpu as pltpu
from jax.sharding import PartitionSpec as P

MESH = pl.DeviceIdType.MESH
F32 = jnp.float32
BF16 = jnp.bfloat16


def tdot(a, b):
    return lax.dot_general(a, b, (((0,), (0,)), ((), ())), preferred_element_type=F32)


def dot(a, b):
    return jnp.dot(a, b, preferred_element_type=F32)


def kernel(
    pairs,
    chunks,
    samples,
    omega,
    diag,
    leaf_piv,
    interp,
    coupling,
    par_piv,
    par_interp,
    far,
    rows_v,
    transfer_v,
    far_done,
    samples_v,
    omega_v,
    diag_v,
    interp_v,
    coup_v,
    par_interp_v,
    far_v,
    leaf_piv_v,
    par_piv_v,
    u_mine,
    u_sib,
    own_q,
    sib_q,
    far_o,
    load_sem,
    coup_sem,
    u_sem,
    z_send,
    z_recv,
    y_send,
    y_recv,
    c_send,
    c_recv,
    ready,
):
    grp, node = lax.axis_index("grp"), lax.axis_index("node")
    pair, parity = node // 2, lax.rem(node, 2)
    node_sib = node + 1 - 2 * parity
    grp_sib = grp + 1 - 2 * lax.rem(grp, 2)
    rank = leaf_piv.shape[1]
    half = rank // 2
    m = omega.shape[0]
    width = omega.shape[1] // chunks
    below, above = pair > 0, pair < pairs - 1
    lower, upper = (grp, node - 2), (grp, node + 2)

    barrier = pltpu.get_barrier_semaphore()

    def greet(where):
        pl.semaphore_signal(barrier, inc=1, device_id=where, device_id_type=MESH)

    greet((grp, node_sib))
    greet((grp_sib, node))
    pl.when(below)(lambda: greet(lower))
    pl.when(above)(lambda: greet(upper))

    loads = []
    for at, (src, dst) in enumerate(
        (
            (interp, interp_v),
            (omega, omega_v),
            (diag, diag_v),
            (samples, samples_v),
            (par_interp, par_interp_v),
            (far, far_v),
            (leaf_piv, leaf_piv_v),
            (par_piv, par_piv_v),
        )
    ):
        loads.append(pltpu.make_async_copy(src, dst, load_sem.at[at]))
    for load in loads[6:] + loads[:4]:
        load.start()

    greeted = 2 + (pair + pairs - 1) // pairs + (2 * pairs - 2 - pair) // pairs
    pl.semaphore_wait(barrier, greeted)

    def remote(src, dst, send, recv, where):
        return pltpu.make_async_remote_copy(
            src_ref=src,
            dst_ref=dst,
            send_sem=send,
            recv_sem=recv,
            device_id=where,
            device_id_type=MESH,
        )

    sent = []

    def send(*where):
        copy = remote(*where)
        copy.start()
        sent.append(copy.wait_send)
        return copy

    coup_copy = send(coupling, coup_v, coup_sem.at[0], coup_sem.at[1], (grp, node_sib))

    def at_distance(d, act):
        pl.when(pair >= d)(lambda: act(pair - d, above, upper))
        pl.when(pair + d < pairs)(lambda: act(pair + d, below, lower))

    def tell(other, onward, where):
        @pl.when(onward)
        def _():
            pl.semaphore_signal(
                ready.at[other], inc=1, device_id=where, device_id_type=MESH
            )

    def heard(other, onward, where):
        pl.semaphore_wait(ready.at[other], 1)
        tell(other, onward, where)

    at_distance(1, tell)

    loads[6].wait()
    loads[7].wait()
    leaf_sel = (lax.broadcasted_iota(jnp.int32, (m, rank), 0) == leaf_piv_v[...]).astype(F32).astype(BF16)
    slots = par_piv_v[pl.ds(pair, 1), :]
    rows = lax.broadcasted_iota(jnp.int32, (rank, rank), 0)
    own_sel = (rows + parity * rank == slots).astype(F32).astype(BF16)
    sib_sel = (rows + (1 - parity) * rank == slots).astype(F32).astype(BF16)
    pick = dot(leaf_sel, own_sel).astype(BF16)

    loads[0].wait()
    loads[1].wait()
    compressed = tdot(interp_v[...], omega_v[...]).astype(BF16)
    loads[2].wait()
    diag_rows = tdot(pick, diag_v[...]).astype(BF16)
    loads[3].wait()
    skeleton = tdot(pick, samples_v[...]) - dot(diag_rows, omega_v[...])
    coup_copy.wait_recv()
    coup_rows = tdot(sib_sel, coup_v[...]).astype(BF16)
    u_copies = []

    def theirs(k):
        return u_mine.at[k, pl.ds(pl.multiple_of((1 - parity) * half, half), half), :]

    for k in range(chunks):
        cols = slice(k * width, (k + 1) * width)
        u_mine[k] = (skeleton[:, cols] - dot(coup_rows, compressed[:, cols])).astype(BF16)
        u_copies.append(
            send(theirs(k), u_sib.at[k], u_sem.at[0, k], u_sem.at[1, k], (grp, node_sib))
        )

    loads[4].start()
    loads[5].start()
    for d in range(2, pairs):
        at_distance(d, heard)
    loads[4].wait()
    transfer_v[...] = dot(interp_v[...], par_interp_v[...]).astype(BF16)

    def place(q, k, p, h=None):
        if h is None:
            return q.at[k, pl.ds(pl.multiple_of(p * rank, rank), rank), :]
        return q.at[k, pl.ds(pl.multiple_of(p * rank + h * half, half), half), :]

    def to_z(k, other):
        spot = place(own_q, k, pair, parity)
        z_here, z_there = z_send.at[k, other], z_recv.at[k, pair]
        return remote(spot, spot, z_here, z_there, (grp, 2 * other + parity))

    def arrive(k, other, sems, h):
        spot = place(own_q, k, other, h)
        at = sems.at[k, other]
        remote(spot, spot, at, at, (grp, node_sib)).wait_recv()
        return spot

    def share(k, other, spot, h, side):
        c_here, c_there = c_send.at[k, other, side], c_recv.at[k, other, side]
        remote(spot, place(sib_q, k, other, h), c_here, c_there, (grp_sib, node)).start()

    def onward(k, other):
        spot = place(own_q, k, other, parity)
        y_here, y_there = y_send.at[k, other], y_recv.at[k, other]
        remote(spot, spot, y_here, y_there, (grp, node_sib)).start()
        share(k, other, spot, parity, 0)

    def from_z(k, other, *_):
        arrive(k, other, z_recv, parity)
        onward(k, other)

    def from_y(k, other):
        spot = arrive(k, other, y_recv, 1 - parity)
        share(k, other, spot, 1 - parity, 1)

    def drain(k, other, *_):
        spot = place(own_q, k, other, parity)
        y_here, y_there = y_send.at[k, other], y_recv.at[k, other]
        remote(spot, spot, y_here, y_there, (grp, node_sib)).wait_send()
        for side in range(2):
            c_here, c_there = c_send.at[k, other, side], c_recv.at[k, other, side]
            remote(spot, spot, c_here, c_there, (grp_sib, node)).wait_send()

    def landed(k, other, *_):
        for side in range(2):
            spot = place(sib_q, k, other, parity)
            at = c_recv.at[k, other, side]
            remote(spot, spot, at, at, (grp_sib, node)).wait_recv()

    for k in range(chunks):
        cols = slice(k * width, (k + 1) * width)
        u_copies[k].wait_recv()
        mine = u_mine[k, pl.ds(pl.multiple_of(parity * half, half), half), :]
        merged = (mine.astype(F32) + u_sib[k].astype(F32)).astype(BF16)
        own_q[k, pl.ds(pl.multiple_of(pair * rank + parity * half, half), half), :] = merged
        rows_v[:, cols] = merged
        for d in range(pairs - 1, 0, -1):
            at_distance(d, lambda other, *_: to_z(k, other).start())
        onward(k, pair)
    for k in range(chunks):
        for d in range(1, pairs):
            at_distance(d, functools.partial(from_z, k))
    loads[5].wait()
    own_width = far.shape[1] // 2
    for k in range(chunks):
        from_y(k, pair)
        for d in range(1, pairs):
            at_distance(d, lambda other, *_: from_y(k, other))
        far_o[k] = dot(far_v[:, :own_width], own_q[k])

    for k in range(chunks):
        cols = slice(k * width, (k + 1) * width)
        landed(k, pair)
        for d in range(1, pairs):
            at_distance(d, functools.partial(landed, k))
        far_done[:, cols] = (far_o[k] + dot(far_v[:, own_width:], sib_q[k])).astype(BF16)
    for wait in sent:
        wait()
    for k in range(chunks):
        drain(k, pair)
        for d in range(1, pairs):
            at_distance(d, lambda other, *_: to_z(k, other).wait_send())
            at_distance(d, functools.partial(drain, k))


def emit(*refs):
    count = len(refs) // 2
    sem = refs[-1]
    copies = [
        pltpu.make_async_copy(refs[at], refs[count + at], sem.at[at]) for at in range(count)
    ]
    for copy in copies:
        copy.start()
    for copy in copies:
        copy.wait()


def shards(chunks, *args):
    samples, omega, diag, leaf_piv, interp, coupling, par_piv, par_interp, far = args
    pairs = lax.axis_size("node") // 2
    rank = leaf_piv.shape[1]
    m, s = omega.shape
    width = s // chunks
    group = pairs * rank
    hbm = pl.BlockSpec(memory_space=pltpu.HBM)
    vmem = pl.BlockSpec(memory_space=pltpu.VMEM)
    dma = pltpu.SemaphoreType.DMA
    shapes = ((rank // 2, s), (m, rank), (m, s))
    held = pl.pallas_call(
        functools.partial(kernel, pairs, chunks),
        out_shape=tuple(pltpu.VMEM(shape, BF16) for shape in shapes),
        in_specs=[hbm] * len(args),
        out_specs=(vmem, vmem, vmem),
        scratch_shapes=[
            pltpu.VMEM((m, s), BF16),
            pltpu.VMEM((m, s), BF16),
            pltpu.VMEM((m, m), BF16),
            pltpu.VMEM((m, rank), BF16),
            pltpu.VMEM((rank, rank), BF16),
            pltpu.VMEM((rank, rank), BF16),
            pltpu.VMEM(far.shape, BF16),
            pltpu.VMEM(leaf_piv.shape, leaf_piv.dtype),
            pltpu.VMEM(par_piv.shape, par_piv.dtype),
            pltpu.VMEM((chunks, rank, width), BF16),
            pltpu.VMEM((chunks, rank // 2, width), BF16),
            pltpu.VMEM((chunks, group, width), BF16),
            pltpu.VMEM((chunks, group, width), BF16),
            pltpu.VMEM((chunks, m, width), F32),
            dma((8,)),
            dma((2,)),
            dma((2, chunks)),
            dma((chunks, pairs)),
            dma((chunks, pairs)),
            dma((chunks, pairs)),
            dma((chunks, pairs)),
            dma((chunks, pairs, 2)),
            dma((chunks, pairs, 2)),
            pltpu.SemaphoreType.REGULAR((pairs,)),
        ],
        compiler_params=pltpu.CompilerParams(
            collective_id=0, has_side_effects=True, vmem_limit_bytes=60 * 1024 * 1024
        ),
        name="merge_level",
    )(*args)
    return pl.pallas_call(
        emit,
        out_shape=tuple(jax.ShapeDtypeStruct(shape, BF16) for shape in shapes),
        in_specs=[pl.BlockSpec(memory_space=pl.ANY)] * len(shapes),
        out_specs=(hbm,) * len(shapes),
        scratch_shapes=[dma((len(shapes),))],
        name="emit",
    )(*(pltpu.with_memory_space_constraint(block, pltpu.VMEM) for block in held))


def solution(mesh):
    split = P(("grp", "node"), None)
    return jax.shard_map(
        functools.partial(shards, 2),
        mesh=mesh,
        in_specs=(split, split, split, split, split, split, P("grp", None), split, split),
        out_specs=(split, split, split),
        check_vma=False,
    )
```
